256 devices in a mesh: tm: 16 (over x_lo, z), heads: 4 (over y), rep: 4 (over x_hi, core).
Axes of the slice: x: 4 (x_hi: 2, x_lo: 2; x = x_hi * 2 + x_lo), y: 4, z: 8, core: 2. Of those that a mesh axis runs over, the one named last changes fastest.
Arguments:
- queries: bfloat16 [16384, 2560], P(('tm', 'rep'), 'heads'), may hold values from -100 to 100
- keys: bfloat16 [16384, 2560], P(('tm', 'rep'), 'heads'), may hold values from -4 to 4
- values: bfloat16 [16384, 2560], P(('tm', 'rep'), 'heads'), may hold values from -6 to 6
- block_lists: int32 [128, 16], P(('tm', 'rep')), may hold values from 0 to 127, as said below
- list_counts: int32 [128], P(('tm', 'rep')), may hold values from 2 to 16, as said below
- out_weight: bfloat16 [2560, 5120], P('heads', 'rep'), may hold values from -0.125 to 0.125
- gate: float32 [5120], P('rep'), may hold values from 0.5 to 2
Outputs:
- branch: bfloat16 [16384, 5120], P(('tm', 'heads'), 'rep')
The draws below stay inside these ranges and needn't reach their ends.
Inputs may be any that keep to these rules, and one draw needn't show every extreme that they name: `block_lists`: entry 0 of block b's list is b itself; only the first list_counts[b] entries count, the rest are arbitrary block numbers. `list_counts`: every draw has a block whose count is 16.
All inputs are finite; a program needn't handle non-finite values.
Results may differ from the reference program's by a relative error of at most 0.0085.
Values may be sent and summed in bfloat16 or wider, within the bound.
No kernel may reach another device: no remote copies, remote signals or barrier semaphores. Data moves between devices by JAX's collectives and lax.ppermute only.
A program may use at most 64 MiB of HBM per device.

```python
import math
import jax
import jax.numpy as jnp
from jax import lax

D = 5120
HD = 128
HEADS = 20
BLOCK = 128
LIST = 16
TOKENS = 16384
QBLOCKS = 128
FRAMES = 16
FRAME_BLOCKS = 8


def list_draw(key):
    base = jax.random.fold_in(key, 23)
    key_dist, key_sign, key_space = jax.random.split(base, 3)
    block_ids = jnp.arange(QBLOCKS, dtype=jnp.int32)
    frame = block_ids // FRAME_BLOCKS
    tries = jax.random.randint(key_dist, (QBLOCKS, LIST, 3), 0, FRAMES)
    distance = jnp.min(tries, axis=2)
    direction = 2 * jax.random.randint(key_sign, (QBLOCKS, LIST), 0, 2) - 1
    target = frame[:, None] + direction * distance
    outside = (target < 0) | (target >= FRAMES)
    target = jnp.where(outside, frame[:, None] - direction * distance, target)
    target = jnp.clip(target, 0, FRAMES - 1)
    spatial = jax.random.randint(key_space, (QBLOCKS, LIST), 0, FRAME_BLOCKS)
    listed = target * FRAME_BLOCKS + spatial
    first_slot = jnp.arange(LIST)[None, :] == 0
    listed = jnp.where(first_slot, block_ids[:, None], listed)
    return listed.astype(jnp.int32)


def count_draw(key):
    base = jax.random.fold_in(key, 31)
    key_frame, key_block, key_pick = jax.random.split(base, 3)
    frame_shift = jax.random.randint(key_frame, (FRAMES,), 0, 3)
    block_shift = jax.random.randint(key_block, (QBLOCKS,), 0, 2)
    block_ids = jnp.arange(QBLOCKS, dtype=jnp.int32)
    shift_total = jnp.minimum(frame_shift[block_ids // FRAME_BLOCKS] + block_shift, 2)
    counts = jnp.maximum(jnp.right_shift(jnp.int32(LIST), shift_total), 2)
    chosen = jax.random.randint(key_pick, (), 0, QBLOCKS)
    counts = jnp.where(block_ids == chosen, LIST, counts)
    return counts.astype(jnp.int32)


def paired_fields(key):
    base = jax.random.fold_in(key, 11)
    key_query, key_key = jax.random.split(base, 2)
    width = HEADS * HD
    key_field = jnp.clip(jax.random.normal(key_key, (TOKENS, width), jnp.float32), -4.0, 4.0)
    query_field = jnp.clip(2.0 * jax.random.normal(key_query, (TOKENS, width), jnp.float32), -8.0, 8.0)
    return (query_field, key_field)


def draw_queries(key, part):
    return paired_fields(key)[0].astype(jnp.bfloat16)


def draw_keys(key, part):
    return paired_fields(key)[1].astype(jnp.bfloat16)


def draw_block_lists(key, part):
    return list_draw(key)


def draw_list_counts(key, part):
    return count_draw(key)


def shard_levels(key, dims, cuts, smallest, top_value):
    gain = 1.0
    for axis_at, parts in cuts:
        heights = jax.random.uniform(jax.random.fold_in(jax.random.fold_in(key, 6), axis_at), (parts,), jnp.float32, smallest / len(cuts), top_value / len(cuts))
        gain = gain * jnp.repeat(jnp.exp(heights), dims[axis_at] // parts).reshape((-1,) + (1,) * (len(dims) - 1 - axis_at))
    return gain


def normal_values(own_key, shape, spread, bound, pieces=(), held_as=jnp.bfloat16):
    entries = spread * jax.random.normal(own_key, shape, jnp.float32)
    if pieces:
        entries = entries * shard_levels(own_key, shape, pieces, -0.22, 0.18)
    return jnp.clip(entries, -bound, bound).astype(held_as)


def setup_inputs(seed: int = 0) -> dict:
    key_of = jax.random.split(jax.random.key(seed), 8)
    return {
        "queries": draw_queries(jax.random.fold_in(key_of[7], 71), 0),
        "keys": draw_keys(jax.random.fold_in(key_of[7], 71), 0),
        "values": normal_values(key_of[2], (TOKENS, HEADS * HD), 1.0, 6.0, ((0, 64), (1, 4))),
        "block_lists": draw_block_lists(jax.random.fold_in(key_of[7], 71), 0),
        "list_counts": draw_list_counts(jax.random.fold_in(key_of[7], 71), 0),
        "out_weight": normal_values(key_of[5], (HEADS * HD, D), (HEADS * HD) ** -0.5, 0.125, ((0, 4), (1, 4))),
        "gate": jnp.clip(jnp.exp(math.log(2.0) - 1.3862944 * jax.random.uniform(key_of[6], (D,), jnp.float32) ** shard_levels(key_of[6], (D,), ((0, 4),), -0.2, 0.2)), 0.5, 2.0),
    }


def reference(queries, keys, values, block_lists, list_counts, out_weight, gate):
    slot_ids = jnp.arange(LIST)
    slot_used = slot_ids[None, :] < list_counts[:, None]
    repeated = (block_lists[:, :, None] == block_lists[:, None, :]) & slot_used[:, None, :] & (slot_ids[None, None, :] < slot_ids[None, :, None])
    fresh = slot_used & jnp.logical_not(jnp.any(repeated, axis=2))
    logit_scale = 1.0 / (HD ** 0.5)

    def one_head(head_index):
        start = (head_index * HD).astype(jnp.int32)
        head_queries = lax.dynamic_slice_in_dim(queries, start, HD, 1).reshape(QBLOCKS, BLOCK, HD).astype(jnp.float32)
        key_head = lax.dynamic_slice_in_dim(keys, start, HD, 1).reshape(QBLOCKS, BLOCK, HD)
        value_head = lax.dynamic_slice_in_dim(values, start, HD, 1).reshape(QBLOCKS, BLOCK, HD)
        gathered_keys = key_head[block_lists].astype(jnp.float32)
        gathered_values = value_head[block_lists].astype(jnp.float32)
        attention_logits = jnp.einsum("zsh,zgyh->zsgy", head_queries, gathered_keys, precision=lax.Precision.HIGHEST) * logit_scale
        masked = jnp.where(fresh[:, None, :, None], attention_logits, -jnp.inf)
        row_max = jnp.max(masked, axis=(2, 3), keepdims=True)
        weights = jnp.exp(masked - row_max)
        denom = jnp.sum(weights, axis=(2, 3))
        rounded_output = lax.optimization_barrier(weights.astype(jnp.bfloat16)).astype(jnp.float32)
        weighted_value_sum = jnp.einsum("pwfh,pfhi->pwi", rounded_output, gathered_values, precision=lax.Precision.HIGHEST)
        return (weighted_value_sum / denom[:, :, None]).reshape(TOKENS, HD)

    per_head = lax.map(one_head, jnp.arange(HEADS, dtype=jnp.int32))
    attended = jnp.transpose(per_head, (1, 0, 2)).reshape(TOKENS, HEADS * HD).astype(jnp.bfloat16)
    projected = jnp.dot(attended, out_weight, preferred_element_type=jnp.float32)
    return (gate.astype(jnp.float32)[None, :] * projected).astype(jnp.bfloat16)
```

```python
import functools
import math

import jax
import jax.numpy as jnp
from jax import lax
from jax.experimental import pallas as pl
from jax.experimental.pallas import tpu as pltpu
from jax.sharding import Mesh, PartitionSpec as P

HD = 128
BLOCK = 128
LIST = 16
HEADS = 5
ROWS = 2 * BLOCK
WIDTH = HEADS * HD
TAIL = 16
EMPTY = -1e30
SCALE2 = math.log2(math.e) / HD**0.5

SOURCES = [(0, 0), (0, 1)] + [(s * d, c) for d in (1, 2, 3) for s in (-1, 1) for c in (0, 1)] + [(4, 0), (4, 1)]


def shift(value, axes, size, steps):
    return lax.ppermute(value, axes, [(i, (i + steps) % size) for i in range(size)])


def shift_x(value, steps):
    at = [2 * (x % 2) + x // 2 for x in range(4)]
    return lax.ppermute(value, ("xlo", "xhi"), [(at[x], at[(x + steps) % 4]) for x in range(4)])


def swap_core(value):
    return lax.ppermute(value, "core", [(0, 1), (1, 0)])


def attention(first_pair, pairs, split, start, last, mask_ref, q_ref, *refs):
    refs = list(refs)
    if not start:
        acc_in, ml_in = refs[:2]
        refs = refs[2:]
    count = pairs * 2 if split else pairs
    sources, refs = refs[:count], refs[count:]
    if last:
        outs, refs = refs[:4], refs[4:]
        acc_ref, ml_ref, refs = refs[0], refs[1], refs[2:]
    else:
        acc_ref, ml_ref, refs = refs[0].at[0], refs[1].at[0], refs[2:]
    kv, sems, scores, top, total, chosen = refs
    qb = pl.program_id(0)

    @pl.when(qb == 0)
    def _():
        copies = []
        for i, source in enumerate(sources):
            target = kv.at[i // 2, i % 2] if split else kv.at[i]
            copies.append(pltpu.make_async_copy(source, target, sems.at[i]))
        for copy in copies:
            copy.start()
        for copy in copies:
            copy.wait()

    n = jnp.int32(0)
    for b in range(2 * pairs):
        chosen[n] = jnp.int32(b)
        n = n + mask_ref[qb, 2 * first_pair + b]

    for h in range(HEADS):
        top[h] = jnp.full((BLOCK, BLOCK), EMPTY, jnp.float32)
        total[h] = jnp.zeros((BLOCK, BLOCK), jnp.float32)

    def first_pass(i, carry):
        b = chosen[i]
        rows = pl.ds(pl.multiple_of((b & 1) * BLOCK, BLOCK), BLOCK)
        for h in range(HEADS):
            cols = slice(h * HD, (h + 1) * HD)
            s = (
                lax.dot_general(
                    q_ref[0, :, cols],
                    kv[b >> 1, 0, rows, cols],
                    (((1,), (1,)), ((), ())),
                    preferred_element_type=jnp.float32,
                )
                * SCALE2
            )
            scores[i, h] = s
            top[h] = jnp.maximum(top[h], s)
        return carry

    lax.fori_loop(0, n, first_pass, 0)

    kept = []
    for h in range(HEADS):
        cols = slice(h * HD, (h + 1) * HD)
        peak = jnp.max(top[h], axis=1, keepdims=True)
        if start:
            acc_ref[:, cols] = jnp.zeros((BLOCK, HD), jnp.float32)
            kept.append((peak, None))
        else:
            old = ml_in[0, :, h : h + 1]
            peak = jnp.maximum(peak, old)
            factor = jnp.exp2(old - peak)
            acc_ref[:, cols] = acc_in[0, :, cols] * factor
            kept.append((peak, ml_in[0, :, 8 + h : 9 + h] * factor))
        top[h] = jnp.broadcast_to(peak, (BLOCK, BLOCK))

    def second_pass(i, carry):
        b = chosen[i]
        rows = pl.ds(pl.multiple_of((b & 1) * BLOCK, BLOCK), BLOCK)
        for h in range(HEADS):
            cols = slice(h * HD, (h + 1) * HD)
            p = jnp.exp2(scores[i, h] - top[h])
            total[h] = total[h] + p
            acc_ref[:, cols] = acc_ref[:, cols] + jnp.dot(
                p.astype(jnp.bfloat16), kv[b >> 1, 1, rows, cols], preferred_element_type=jnp.float32
            )
        return carry

    lax.fori_loop(0, n, second_pass, 0)

    lane = lax.broadcasted_iota(jnp.int32, (BLOCK, BLOCK), 1)
    if not last:
        table = jnp.zeros((BLOCK, BLOCK), jnp.float32)
        for h in range(HEADS):
            peak, old = kept[h]
            weight = jnp.sum(total[h], axis=1, keepdims=True)
            weight = weight if old is None else weight + old
            table = jnp.where(lane == h, peak, table)
            table = jnp.where(lane == 8 + h, weight, table)
        ml_ref[...] = table
        return

    table = jnp.zeros((BLOCK, BLOCK), jnp.float32)
    rest = jnp.zeros((BLOCK, BLOCK), jnp.float32)
    done = []
    for h in range(HEADS):
        cols = slice(h * HD, (h + 1) * HD)
        peak, old = kept[h]
        weight = jnp.sum(total[h], axis=1, keepdims=True)
        weight = weight if old is None else weight + old
        some = weight > 0.0
        weight = jnp.where(some, weight, 1.0)
        done.append((acc_ref[:, cols] / weight).astype(jnp.bfloat16))
        lse = jnp.where(some, peak + jnp.log2(weight), EMPTY)
        high = lse.astype(jnp.bfloat16).astype(jnp.float32)
        middle = (lse - high).astype(jnp.bfloat16).astype(jnp.float32)
        low = (lse - high - middle).astype(jnp.bfloat16).astype(jnp.float32)
        table = jnp.where(lane == h, high, table)
        table = jnp.where(lane == 8 + h, middle, table)
        rest = jnp.where(lane == h, low, rest)
    row_table = table.T[0:TAIL].astype(jnp.bfloat16)
    row_rest = rest.T[0:TAIL].astype(jnp.bfloat16)
    for r in range(4):
        for b in range(2):

            @pl.when(qb == 2 * r + b)
            def _(r=r, b=b):
                for h in range(HEADS):
                    outs[r][b * BLOCK : (b + 1) * BLOCK, h * HD : (h + 1) * HD] = done[h]
                outs[r][ROWS : ROWS + TAIL, b * BLOCK : (b + 1) * BLOCK] = row_table
                outs[r][ROWS : ROWS + TAIL, ROWS + b * BLOCK : ROWS + (b + 1) * BLOCK] = row_rest
                if b == 1:
                    outs[r][ROWS : ROWS + TAIL, 4 * BLOCK : WIDTH] = jnp.zeros((TAIL, WIDTH - 4 * BLOCK), jnp.bfloat16)


def attend(mask, queries, state, sources, first_pair, pairs, last):
    start = state is None
    split = len(sources) == 2 * pairs
    one = lambda i, m: (i, 0, 0)
    state_specs = [pl.BlockSpec((1, BLOCK, WIDTH), one), pl.BlockSpec((1, BLOCK, BLOCK), one)]
    state_shapes = [
        jax.ShapeDtypeStruct((8, BLOCK, WIDTH), jnp.float32),
        jax.ShapeDtypeStruct((8, BLOCK, BLOCK), jnp.float32),
    ]
    scratch = [
        pltpu.VMEM((pairs, 2, ROWS, WIDTH), jnp.bfloat16),
        pltpu.SemaphoreType.DMA((len(sources),)),
        pltpu.VMEM((2 * pairs, HEADS, BLOCK, BLOCK), jnp.float32),
        pltpu.VMEM((HEADS, BLOCK, BLOCK), jnp.float32),
        pltpu.VMEM((HEADS, BLOCK, BLOCK), jnp.float32),
        pltpu.SMEM((2 * pairs,), jnp.int32),
    ]
    if last:
        out_specs = [pl.BlockSpec((ROWS + TAIL, WIDTH), lambda i, m: (0, 0))] * 4
        out_shape = [jax.ShapeDtypeStruct((ROWS + TAIL, WIDTH), jnp.bfloat16)] * 4
        scratch = [pltpu.VMEM((BLOCK, WIDTH), jnp.float32), pltpu.VMEM((BLOCK, BLOCK), jnp.float32)] + scratch
    else:
        out_specs, out_shape = state_specs, state_shapes
    return pl.pallas_call(
        functools.partial(attention, first_pair, pairs, split, start, last),
        grid_spec=pltpu.PrefetchScalarGridSpec(
            num_scalar_prefetch=1,
            grid=(8,),
            in_specs=[pl.BlockSpec((1, BLOCK, WIDTH), one)]
            + ([] if start else state_specs)
            + [pl.BlockSpec(memory_space=pl.ANY)] * len(sources),
            out_specs=out_specs,
            scratch_shapes=scratch,
        ),
        out_shape=out_shape,
        cost_estimate=pl.CostEstimate(
            flops=pairs * 4 * 5 * 4 * BLOCK**3, transcendentals=pairs * 4 * 5 * BLOCK**2, bytes_accessed=pairs * 2**20
        ),
        name=f"attend{first_pair}",
    )(mask, queries, *(state or ()), *sources)


def combine_kernel(own, one, two, three, out):
    parts = (own, one, two, three)
    for b in range(2):
        rows = slice(b * BLOCK, (b + 1) * BLOCK)
        lses = []
        for part in parts:
            table = part[ROWS : ROWS + TAIL, rows].astype(jnp.float32)
            rest = part[ROWS : ROWS + TAIL, ROWS + b * BLOCK : ROWS + (b + 1) * BLOCK].astype(jnp.float32)
            lses.append(table[0:8] + table[8:16] + rest[0:8])
        peak = functools.reduce(jnp.maximum, lses)
        shares = [jnp.exp2(lse - peak) for lse in lses]
        whole = shares[0] + shares[1] + shares[2] + shares[3]
        shares = jnp.concatenate([share / whole for share in shares], axis=0)
        columns = jnp.concatenate([shares] * 4, axis=0).T
        for h in range(HEADS):
            cols = slice(h * HD, (h + 1) * HD)
            value = jnp.zeros((BLOCK, HD), jnp.float32)
            for j, part in enumerate(parts):
                value = value + part[rows, cols].astype(jnp.float32) * columns[:, 8 * j + h : 8 * j + h + 1]
            out[rows, cols] = value.astype(jnp.bfloat16)


def combine(parts):
    return pl.pallas_call(
        combine_kernel,
        out_shape=jax.ShapeDtypeStruct((ROWS, WIDTH), jnp.bfloat16),
        name="combine",
    )(*parts)


def project_kernel(place_ref, a, b, c, d, w0, w1, w2, w2b, w3, gate, out, rows):
    @pl.when(pl.program_id(0) == 0)
    def _():
        for j, piece in enumerate((a, b, c, d)):
            rows[place_ref[j]] = piece[...]

    cut = w2.shape[0]
    dot = functools.partial(jnp.dot, preferred_element_type=jnp.float32)
    value = dot(rows[0], w0[...]) + dot(rows[1], w1[...]) + dot(rows[3], w3[...])
    value = value + dot(rows[2, :, :cut], w2[...]) + dot(rows[2, :, cut:], w2b[...])
    out[...] = (gate[...] * value).astype(jnp.bfloat16)


def project(place, pieces, weights, gate):
    cols = weights[0].shape[1]
    tile = 256
    whole = pl.BlockSpec((ROWS, WIDTH), lambda i, m: (0, 0))
    return pl.pallas_call(
        project_kernel,
        grid_spec=pltpu.PrefetchScalarGridSpec(
            num_scalar_prefetch=1,
            grid=(cols // tile,),
            in_specs=[whole] * 4
            + [pl.BlockSpec((w.shape[0], tile), lambda i, m: (0, i)) for w in weights]
            + [pl.BlockSpec((1, tile), lambda i, m: (0, i))],
            out_specs=pl.BlockSpec((ROWS, tile), lambda i, m: (0, i)),
            scratch_shapes=[pltpu.VMEM((4, ROWS, WIDTH), jnp.bfloat16)],
        ),
        out_shape=jax.ShapeDtypeStruct((ROWS, cols), jnp.bfloat16),
        name="project",
    )(place, *pieces, *weights, gate[None, :])


CUT = 384


def shards(queries, keys, values, block_lists, list_counts, out_weight, gate):
    xlo, z, y = lax.axis_index("xlo"), lax.axis_index("z"), lax.axis_index("y")
    xhi, core = lax.axis_index("xhi"), lax.axis_index("core")

    own = jnp.stack([keys, values])
    before, after = [own], [own]
    for _ in range(3):
        before.append(shift(before[-1], "z", 8, 1))
        after.append(shift(after[-1], "z", 8, -1))
    far_keys = shift(before[3][0], "z", 8, 1)
    far_values = shift(after[3][1], "z", 8, -1)
    w1, w3 = shift(out_weight, "y", 4, 1), shift(out_weight, "y", 4, -1)
    weights = [out_weight, w1, shift(w1[:CUT], "y", 4, 1), shift(w3[CUT:], "y", 4, -1), w3]

    table = jnp.concatenate([block_lists, list_counts[:, None]], axis=1)
    tables = jnp.stack([table] + [shift_x(table, r) for r in (1, 2, 3)]).reshape(8, LIST + 1)
    all_queries = jnp.stack([queries] + [shift_x(queries, r) for r in (1, 2, 3)]).reshape(8, BLOCK, WIDTH)

    steps = jnp.array([s for s, _ in SOURCES], jnp.int32)
    other = jnp.array([c for _, c in SOURCES], jnp.int32)
    quarter = 2 * xhi + jnp.bitwise_xor(other, core)
    first = ((xlo * 8 + (z + steps) % 8) * 4 + quarter) * 2
    ids = (first[:, None] + jnp.arange(2)[None, :]).reshape(-1)
    used = jnp.arange(LIST)[None, :] < tables[:, LIST:]
    mask = jnp.any((tables[:, :LIST, None] == ids[None, None, :]) & used[:, :, None], axis=1).astype(jnp.int32)

    near = [own, swap_core(own)]
    for d in (1, 2, 3):
        near += [before[d], swap_core(before[d]), after[d], swap_core(after[d])]
    state = attend(mask, all_queries, None, near[:6], 0, 6, False)
    state = attend(mask, all_queries, state, near[6:], 6, 8, False)
    far = [far_keys, far_values, swap_core(far_keys), swap_core(far_values)]
    parts = attend(mask, all_queries, state, far, 14, 2, True)

    back = [parts[0]] + [shift_x(parts[r], -r) for r in (1, 2, 3)]
    attended = combine(back)

    places = [(i, j) for i in range(4) for j in range(4)]
    here = lax.ppermute(attended, ("y", "xhi", "core"), [(4 * i + j, 4 * j + i) for i, j in places])
    there = lax.ppermute(attended, ("y", "xhi", "core"), [(4 * i + j, 4 * j + (i ^ 2)) for i, j in places])
    pieces = [here, there, swap_core(here), swap_core(there)]
    groups = jnp.stack([2 * xhi + core, 2 * (1 - xhi) + core, 2 * xhi + 1 - core, 2 * (1 - xhi) + 1 - core])
    place = ((y - groups) % 4).astype(jnp.int32)
    return project(place, pieces, weights, gate)


def solution(mesh):
    fine = Mesh(mesh.devices.reshape(2, 8, 4, 2, 2), ("xlo", "z", "y", "xhi", "core"))
    rows, rep = ("xlo", "z", "xhi", "core"), ("xhi", "core")
    placed = (P(rows, "y"), P(rows, "y"), P(rows, "y"), P(rows, None), P(rows), P("y", rep), P(rep))
    return jax.shard_map(
        shards, mesh=fine, in_specs=placed, out_specs=P(("xlo", "z", "y"), rep), check_vma=False
    )
```

```python
import functools
import math

import jax
import jax.numpy as jnp
from jax import lax
from jax.experimental import pallas as pl
from jax.experimental.pallas import tpu as pltpu
from jax.sharding import Mesh, PartitionSpec as P


HD = 128
BLOCK = 128
LIST = 16
HEADS = 5
ROWS = 2 * BLOCK
WIDTH = HEADS * HD
TAIL = 32
EMPTY = -1e30
SCALE2 = math.log2(math.e) / HD**0.5

SOURCES = [(0, 0), (0, 1)] + [(s * d, c) for d in (1, 2, 3) for s in (-1, 1) for c in (0, 1)] + [(4, 0), (4, 1)]


def shift(value, axes, size, steps):
    return lax.ppermute(value, axes, [(i, (i + steps) % size) for i in range(size)])


def shift_x(value, steps):
    at = [2 * (x % 2) + x // 2 for x in range(4)]
    return lax.ppermute(value, ("xlo", "xhi"), [(at[x], at[(x + steps) % 4]) for x in range(4)])


def swap_core(value):
    return lax.ppermute(value, "core", [(0, 1), (1, 0)])


def prepare_kernel(keys, values, out):
    for b in range(2):
        rows = slice(b * BLOCK, (b + 1) * BLOCK)
        for h in range(HEADS):
            cols = slice(h * HD, (h + 1) * HD)
            out[0, b * HEADS + h] = keys[rows, cols]
            out[1, b * HEADS + h] = values[rows, cols].T


def prepare(keys, values):
    return pl.pallas_call(
        prepare_kernel,
        out_shape=jax.ShapeDtypeStruct((2, 2 * HEADS, BLOCK, HD), jnp.bfloat16),
        name="prepare",
    )(keys, values)


def attention(first_pair, pairs, split, start, last, mask_ref, *refs):
    refs = list(refs)
    if not start:
        acc_in, ml_in = refs[:2]
        refs = refs[2:]
    sent, refs = refs[:4], refs[4:]
    count = pairs * 2 if split else pairs
    sources, refs = refs[:count], refs[count:]
    if last:
        outs, refs = refs[:4], refs[4:]
        acc_ref, part, out_sems, refs = refs[0], refs[1], refs[2], refs[3:]
    else:
        acc_ref, ml_ref, refs = refs[0].at[0], refs[1].at[0], refs[2:]
    q, kv, sems, scores, chosen = refs
    qb = pl.program_id(0)

    @pl.when(qb == 0)
    def _():
        copies = []
        for i, source in enumerate(sources):
            target = kv.at[i // 2, i % 2] if split else kv.at[i]
            copies.append(pltpu.make_async_copy(source, target, sems.at[i]))
        for i, source in enumerate(sent):
            copies.append(pltpu.make_async_copy(source, q.at[i], sems.at[count + i]))
        for copy in copies:
            copy.start()
        for copy in copies:
            copy.wait()

    n = jnp.int32(0)
    for b in range(2 * pairs):
        chosen[n] = jnp.int32(b)
        n = n + mask_ref[qb, 2 * first_pair + b]

    q_rows = pl.ds(pl.multiple_of((qb & 1) * BLOCK, BLOCK), BLOCK)

    def first_pass(i, tops):
        b = chosen[i]
        pair, tile = b >> 1, (b & 1) * HEADS
        new = []
        for h in range(HEADS):
            s = (
                lax.dot_general(
                    kv[pair, 0, tile + h],
                    q[qb >> 1, q_rows, h * HD : (h + 1) * HD],
                    (((1,), (1,)), ((), ())),
                    preferred_element_type=jnp.float32,
                )
                * SCALE2
            )
            scores[i, h] = s
            new.append(jnp.maximum(tops[h], jnp.max(s.reshape(16, 8, BLOCK), axis=0)))
        return tuple(new)

    tops = lax.fori_loop(0, n, first_pass, (jnp.full((8, BLOCK), EMPTY, jnp.float32),) * HEADS)

    peaks, olds = [], []
    for h in range(HEADS):
        rows = slice(h * HD, (h + 1) * HD)
        peak = jnp.max(tops[h], axis=0, keepdims=True)
        if start:
            acc_ref[rows, :] = jnp.zeros((HD, BLOCK), jnp.float32)
            olds.append(None)
        else:
            old = ml_in[0, h : h + 1, :]
            peak = jnp.maximum(peak, old)
            factor = jnp.exp2(old - peak)
            acc_ref[rows, :] = acc_in[0, rows, :] * factor
            olds.append(ml_in[0, 8 + h : 9 + h, :] * factor)
        peaks.append(peak)

    def second_pass(i, totals):
        b = chosen[i]
        pair, tile = b >> 1, (b & 1) * HEADS
        new = []
        for h in range(HEADS):
            rows = slice(h * HD, (h + 1) * HD)
            p = jnp.exp2(scores[i, h] - peaks[h])
            new.append(totals[h] + jnp.sum(p.reshape(16, 8, BLOCK), axis=0))
            acc_ref[rows, :] = acc_ref[rows, :] + jnp.dot(
                kv[pair, 1, tile + h], p.astype(jnp.bfloat16), preferred_element_type=jnp.float32
            )
        return tuple(new)

    totals = lax.fori_loop(0, n, second_pass, (jnp.zeros((8, BLOCK), jnp.float32),) * HEADS)

    line = lax.broadcasted_iota(jnp.int32, (8, BLOCK), 0)
    zero = jnp.zeros((8, BLOCK), jnp.float32)
    weights = []
    for h in range(HEADS):
        weight = jnp.sum(totals[h], axis=0, keepdims=True)
        weights.append(weight if olds[h] is None else weight + olds[h])
    if not last:
        tops_table, sums_table = zero, zero
        for h in range(HEADS):
            tops_table = jnp.where(line == h, peaks[h], tops_table)
            sums_table = jnp.where(line == h, weights[h], sums_table)
        ml_ref[0:8, :] = tops_table
        ml_ref[8:16, :] = sums_table
        return

    tables = [zero, zero, zero, zero]
    for h in range(HEADS):
        rows = slice(h * HD, (h + 1) * HD)
        some = weights[h] > 0.0
        weight = jnp.where(some, weights[h], 1.0)
        part[qb, rows, :] = (acc_ref[rows, :] * (1.0 / weight)).astype(jnp.bfloat16)
        lse = jnp.where(some, peaks[h] + jnp.log2(weight), EMPTY)
        for j in range(3):
            piece = lse.astype(jnp.bfloat16).astype(jnp.float32)
            tables[j] = jnp.where(line == h, piece, tables[j])
            lse = lse - piece
    part[qb, WIDTH : WIDTH + TAIL, :] = jnp.concatenate(tables, axis=0).astype(jnp.bfloat16)

    copies = [pltpu.make_async_copy(part.at[pl.ds(2 * r, 2)], outs[r], out_sems.at[r]) for r in range(4)]
    for r in range(4):
        pl.when(qb == 2 * r + 1)(copies[r].start)

    @pl.when(qb == 7)
    def _():
        for copy in copies:
            copy.wait()


def attend(mask, queries, state, sources, first_pair, pairs, last):
    start = state is None
    split = len(sources) == 2 * pairs
    one = lambda i, m: (i, 0, 0)
    state_specs = [pl.BlockSpec((1, WIDTH, BLOCK), one), pl.BlockSpec((1, 16, BLOCK), one)]
    state_shapes = [
        jax.ShapeDtypeStruct((8, WIDTH, BLOCK), jnp.float32),
        jax.ShapeDtypeStruct((8, 16, BLOCK), jnp.float32),
    ]
    scratch = [
        pltpu.VMEM((4, ROWS, WIDTH), jnp.bfloat16),
        pltpu.VMEM((pairs, 2, 2 * HEADS, BLOCK, HD), jnp.bfloat16),
        pltpu.SemaphoreType.DMA((len(sources) + 4,)),
        pltpu.VMEM((2 * pairs, HEADS, BLOCK, BLOCK), jnp.float32),
        pltpu.SMEM((2 * pairs,), jnp.int32),
    ]
    anywhere = pl.BlockSpec(memory_space=pl.ANY)
    if last:
        out_specs = [anywhere] * 4
        out_shape = [jax.ShapeDtypeStruct((2, WIDTH + TAIL, BLOCK), jnp.bfloat16)] * 4
        scratch = [
            pltpu.VMEM((WIDTH, BLOCK), jnp.float32),
            pltpu.VMEM((8, WIDTH + TAIL, BLOCK), jnp.bfloat16),
            pltpu.SemaphoreType.DMA((4,)),
        ] + scratch
    else:
        out_specs, out_shape = state_specs, state_shapes
    return pl.pallas_call(
        functools.partial(attention, first_pair, pairs, split, start, last),
        grid_spec=pltpu.PrefetchScalarGridSpec(
            num_scalar_prefetch=1,
            grid=(8,),
            in_specs=([] if start else state_specs) + [anywhere] * (4 + len(sources)),
            out_specs=out_specs,
            scratch_shapes=scratch,
        ),
        out_shape=out_shape,
        cost_estimate=pl.CostEstimate(
            flops=4 * 10**9, transcendentals=pairs * 4 * 5 * BLOCK**2, bytes_accessed=pairs * 2**20
        ),
    )(mask, *(state or ()), *queries, *sources)


def combine_kernel(own, one, two, three, out):
    parts = (own, one, two, three)
    for b in range(2):
        lses = []
        for part in parts:
            table = part[b, WIDTH : WIDTH + TAIL, :].astype(jnp.float32)
            lses.append(table[0:8] + table[8:16] + table[16:24])
        peak = functools.reduce(jnp.maximum, lses)
        shares = [jnp.exp2(lse - peak) for lse in lses]
        whole = 1.0 / (shares[0] + shares[1] + shares[2] + shares[3])
        shares = [share * whole for share in shares]
        for h in range(HEADS):
            rows = slice(h * HD, (h + 1) * HD)
            value = parts[0][b, rows, :].astype(jnp.float32) * shares[0][h : h + 1]
            for part, share in zip(parts[1:], shares[1:]):
                value = value + part[b, rows, :].astype(jnp.float32) * share[h : h + 1]
            out[b * BLOCK : (b + 1) * BLOCK, rows] = value.T.astype(jnp.bfloat16)


def combine(parts):
    return pl.pallas_call(
        combine_kernel,
        out_shape=jax.ShapeDtypeStruct((ROWS, WIDTH), jnp.bfloat16),
        name="combine",
    )(*parts)


def project_kernel(place_ref, a, b, c, d, w0, t1, b1, t2, b2, t3, b3, gate, out, rows):
    for j, piece in enumerate((a, b, c, d)):
        rows[place_ref[j]] = piece[...]
    dot = functools.partial(jnp.dot, preferred_element_type=jnp.float32)
    for i in range(out.shape[1] // 256):
        cols = slice(i * 256, (i + 1) * 256)
        value = dot(rows[0], w0[:, cols])
        for j, (top, bottom) in enumerate(((t1, b1), (t2, b2), (t3, b3))):
            value = value + dot(rows[j + 1, :, :CUT], top[:, cols])
            value = value + dot(rows[j + 1, :, CUT:], bottom[:, cols])
        out[:, cols] = (gate[:, cols] * value).astype(jnp.bfloat16)


def project(place, pieces, weights, gate):
    cols = weights[0].shape[1]
    vmem = pl.BlockSpec(memory_space=pltpu.VMEM)
    return pl.pallas_call(
        project_kernel,
        in_specs=[pl.BlockSpec(memory_space=pltpu.SMEM)] + [vmem] * (4 + len(weights) + 1),
        out_specs=vmem,
        scratch_shapes=[pltpu.VMEM((4, ROWS, WIDTH), jnp.bfloat16)],
        out_shape=jax.ShapeDtypeStruct((ROWS, cols), jnp.bfloat16),
        name="project",
    )(place, *pieces, *weights, gate[None, :])


CUT = 384


def stages(queries, keys, values, block_lists, list_counts, out_weight, gate):
    xlo, z, y = lax.axis_index("xlo"), lax.axis_index("z"), lax.axis_index("y")
    xhi, core = lax.axis_index("xhi"), lax.axis_index("core")

    own = prepare(keys, values)
    before, after, near = [own], [own], [own]
    near.append(swap_core(own))
    for d in (1, 2, 3):
        before.append(shift(before[-1], "z", 8, 1))
        after.append(shift(after[-1], "z", 8, -1))
        near += [before[d], swap_core(before[d])]
        near += [after[d], swap_core(after[d])]
    far_keys = shift(before[3][0], "z", 8, 1)
    far_values = shift(after[3][1], "z", 8, -1)
    far = [far_keys, far_values, swap_core(far_keys)]
    far.append(swap_core(far_values))

    top, bottom = out_weight[:CUT], out_weight[CUT:]
    t1 = shift(top, "y", 4, 1)
    b3 = shift(bottom, "y", 4, -1)
    b1 = shift(bottom, "y", 4, 1)
    t3 = shift(top, "y", 4, -1)
    t2 = shift(t1, "y", 4, 1)
    b2 = shift(b3, "y", 4, -1)
    weights = [out_weight, t1, b1, t2, b2, t3, b3]

    table = jnp.concatenate([block_lists, list_counts[:, None]], axis=1)
    tables, all_queries = [table], [queries]
    for r in (1, 2, 3):
        tables.append(shift_x(table, r))
        all_queries.append(shift_x(queries, r))
    tables = jnp.stack(tables).reshape(8, LIST + 1)

    steps = jnp.array([s for s, _ in SOURCES], jnp.int32)
    other = jnp.array([c for _, c in SOURCES], jnp.int32)
    quarter = 2 * xhi + jnp.bitwise_xor(other, core)
    first = ((xlo * 8 + (z + steps) % 8) * 4 + quarter) * 2
    ids = (first[:, None] + jnp.arange(2)[None, :]).reshape(-1)
    used = jnp.arange(LIST)[None, :] < tables[:, LIST:]
    mask = jnp.any((tables[:, :LIST, None] == ids[None, None, :]) & used[:, :, None], axis=1).astype(jnp.int32)

    state = attend(mask, all_queries, None, near[:6], 0, 6, False)
    state = attend(mask, all_queries, state, near[6:10], 6, 4, False)
    state = attend(mask, all_queries, state, near[10:], 10, 4, False)
    parts = attend(mask, all_queries, state, far, 14, 2, True)

    back = [parts[0]]
    for r in (1, 2, 3):
        back.append(shift_x(parts[r], -r))
    attended = combine(back)

    places = [(i, j) for i in range(4) for j in range(4)]
    here = lax.ppermute(attended, ("y", "xhi", "core"), [(4 * i + j, 4 * j + i) for i, j in places])
    there = lax.ppermute(attended, ("y", "xhi", "core"), [(4 * i + j, 4 * j + (i ^ 2)) for i, j in places])
    pieces = [here, there, swap_core(here)]
    pieces.append(swap_core(there))
    groups = jnp.stack([2 * xhi + core, 2 * (1 - xhi) + core, 2 * xhi + 1 - core, 2 * (1 - xhi) + 1 - core])
    place = ((y - groups) % 4).astype(jnp.int32)
    return project(place, pieces, weights, gate)


def solution(mesh):
    fine = Mesh(mesh.devices.reshape(2, 8, 4, 2, 2), ("xlo", "z", "y", "xhi", "core"))
    rows, rep = ("xlo", "z", "xhi", "core"), ("xhi", "core")
    placed = (P(rows, "y"), P(rows, "y"), P(rows, "y"), P(rows, None), P(rows), P("y", rep), P(rep))
    return jax.shard_map(stages, mesh=fine, in_specs=placed, out_specs=P(("xlo", "z", "y"), rep), check_vma=False)
```

```python
import functools
import math

import jax
import jax.numpy as jnp
from jax import lax
from jax.experimental import pallas as pl
from jax.experimental.pallas import tpu as pltpu
from jax.sharding import Mesh, PartitionSpec as P


HD = 128
BLOCK = 128
LIST = 16
HEADS = 5
ROWS = 2 * BLOCK
WIDTH = HEADS * HD
TAIL = 32
EMPTY = -1e30
SCALE2 = math.log2(math.e) / HD**0.5

SOURCES = [(0, 0), (0, 1)] + [(s * d, c) for d in (1, 2, 3) for s in (-1, 1) for c in (0, 1)] + [(4, 0), (4, 1)]


def shift(value, axes, size, steps):
    return lax.ppermute(value, axes, [(i, (i + steps) % size) for i in range(size)])


def shift_x(value, steps):
    at = [2 * (x % 2) + x // 2 for x in range(4)]
    return lax.ppermute(value, ("xlo", "xhi"), [(at[x], at[(x + steps) % 4]) for x in range(4)])


def swap_core(value):
    return lax.ppermute(value, "core", [(0, 1), (1, 0)])


def prepare_kernel(keys, values, out):
    for b in range(2):
        rows = slice(b * BLOCK, (b + 1) * BLOCK)
        for h in range(HEADS):
            cols = slice(h * HD, (h + 1) * HD)
            out[0, b * HEADS + h] = keys[rows, cols]
            out[1, b * HEADS + h] = values[rows, cols].T


def prepare(keys, values):
    return pl.pallas_call(
        prepare_kernel,
        out_shape=jax.ShapeDtypeStruct((2, 2 * HEADS, BLOCK, HD), jnp.bfloat16),
        name="prepare",
    )(keys, values)


def attention(first_pair, pairs, split, start, last, heads, mask_ref, *refs):
    refs = list(refs)
    if not start:
        acc_in, ml_in = refs[:2]
        refs = refs[2:]
    sent, refs = refs[:4], refs[4:]
    count = pairs * 2 if split else pairs
    sources, refs = refs[:count], refs[count:]
    outs, refs = (refs[:4], refs[4:]) if last else (refs[:2], refs[2:])
    q, kv, acc, sems, scores, tops, totals, ml, slots, blocks, counts = refs[:11]
    size = len(heads)
    height = size * HD

    copies = []
    for i, source in enumerate(sources):
        target = kv.at[i // 2, i % 2] if split else kv.at[i]
        copies.append(pltpu.make_async_copy(source, target, sems.at[i]))
    for i, source in enumerate(sent):
        copies.append(pltpu.make_async_copy(source, q.at[i], sems.at[count + i]))
    for copy in copies:
        copy.start()
    if not start:
        state = pltpu.make_async_copy(
            acc_in.at[:, heads[0] * HD : heads[0] * HD + height, :], acc.at[0:8], sems.at[count + 4]
        )
        state.start()

    n = jnp.int32(0)
    for i in range(8):
        before = n
        for b in range(2 * pairs):
            slots[n] = jnp.int32(i)
            blocks[n] = jnp.int32(b)
            n = n + mask_ref[i, 2 * first_pair + b]
        counts[i] = n - before
    slots[n] = jnp.int32(8)
    blocks[n] = jnp.int32(0)
    trips = (n + 1) >> 1
    tops[...] = jnp.full(tops.shape, EMPTY, jnp.float32)
    totals[...] = jnp.zeros(totals.shape, jnp.float32)
    if start:
        acc[...] = jnp.zeros(acc.shape, jnp.float32)
    for copy in copies:
        copy.wait()

    def first_pass(j, carry):
        for u in range(2):
            i = 2 * j + u
            slot, b = slots[i], blocks[i]
            at = slot & 7
            pair, tile = b >> 1, (b & 1) * HEADS
            q_rows = pl.ds(pl.multiple_of((at & 1) * BLOCK, BLOCK), BLOCK)
            for k, h in enumerate(heads):
                s = (
                    lax.dot_general(
                        kv[pair, 0, tile + h],
                        q[at >> 1, q_rows, h * HD : (h + 1) * HD],
                        (((1,), (1,)), ((), ())),
                        preferred_element_type=jnp.float32,
                    )
                    * SCALE2
                )
                scores[i, k] = s
                tops[slot, k] = jnp.maximum(tops[slot, k], jnp.max(s.reshape(16, 8, BLOCK), axis=0))
        return carry

    lax.fori_loop(0, trips, first_pass, 0)
    if not start:
        state.wait()
    line = lax.broadcasted_iota(jnp.int32, (8, BLOCK), 0)

    def middle(i, carry):
        peak = jnp.full((8, BLOCK), EMPTY, jnp.float32) if start else ml_in[0, i]
        old = peak
        for k, h in enumerate(heads):
            top = jnp.max(tops[i, k], axis=0, keepdims=True)
            peak = jnp.where(line == h, jnp.maximum(peak, top), peak)
        ml[0, i] = peak
        if not start:
            factor = jnp.exp2(old - peak)
            ml[1, i] = ml_in[1, i] * factor

            @pl.when(counts[i] > 0)
            def _():
                for k, h in enumerate(heads):
                    rows = slice(k * HD, (k + 1) * HD)
                    acc[i, rows, :] = acc[i, rows, :] * factor[h : h + 1]

        return carry

    lax.fori_loop(0, 8, middle, 0)

    def second_pass(j, carry):
        for u in range(2):
            i = 2 * j + u
            slot, b = slots[i], blocks[i]
            pair, tile = b >> 1, (b & 1) * HEADS
            for k, h in enumerate(heads):
                rows = slice(k * HD, (k + 1) * HD)
                p = jnp.exp2(scores[i, k] - ml[0, slot, h : h + 1, :])
                totals[slot, k] = totals[slot, k] + jnp.sum(p.reshape(16, 8, BLOCK), axis=0)
                acc[slot, rows, :] = acc[slot, rows, :] + jnp.dot(
                    kv[pair, 1, tile + h], p.astype(jnp.bfloat16), preferred_element_type=jnp.float32
                )
        return carry

    lax.fori_loop(0, trips, second_pass, 0)

    if not last:
        acc_out, ml_out = outs
        leave = pltpu.make_async_copy(acc.at[0:8], acc_out, sems.at[count + 4])
        leave.start()

    def sums(i):
        weight = jnp.zeros((8, BLOCK), jnp.float32) if start else ml[1, i]
        for k, h in enumerate(heads):
            total = jnp.sum(totals[i, k], axis=0, keepdims=True)
            weight = jnp.where(line == h, weight + total, weight)
        return weight

    if not last:

        def finish(i, carry):
            ml_out[0, i] = ml[0, i]
            ml_out[1, i] = sums(i)
            return carry

        lax.fori_loop(0, 8, finish, 0)
        leave.wait()
        return

    part, out_sems = refs[11:]
    leaves = []
    for r in range(4):
        for i in (2 * r, 2 * r + 1):
            weight = sums(i)
            some = weight > 0.0
            weight = jnp.where(some, weight, 1.0)
            lse = jnp.where(some, ml[0, i] + jnp.log2(weight), EMPTY)
            scale = 1.0 / weight
            for k, h in enumerate(heads):
                rows = slice(k * HD, (k + 1) * HD)
                part[i, rows, :] = (acc[i, rows, :] * scale[h : h + 1]).astype(jnp.bfloat16)
            tables = []
            for _ in range(3):
                piece = lse.astype(jnp.bfloat16).astype(jnp.float32)
                tables.append(piece)
                lse = lse - piece
            tables.append(jnp.zeros((8, BLOCK), jnp.float32))
            part[i, height : height + TAIL, :] = jnp.concatenate(tables, axis=0).astype(jnp.bfloat16)
        leaves.append(pltpu.make_async_copy(part.at[2 * r : 2 * r + 2], outs[r], out_sems.at[r]))
        leaves[-1].start()
    for leave in leaves:
        leave.wait()


def attend(mask, queries, state, sources, first_pair, pairs, heads=None):
    start, last = state is None, heads is not None
    heads = heads or tuple(range(HEADS))
    split = len(sources) == 2 * pairs
    height = len(heads) * HD
    limit = 16 * pairs + 2
    scratch = [
        pltpu.VMEM((4, ROWS, WIDTH), jnp.bfloat16),
        pltpu.VMEM((pairs, 2, 2 * HEADS, BLOCK, HD), jnp.bfloat16),
        pltpu.VMEM((9, height, BLOCK), jnp.float32),
        pltpu.SemaphoreType.DMA((len(sources) + 5,)),
        pltpu.VMEM((limit, len(heads), BLOCK, BLOCK), jnp.float32),
        pltpu.VMEM((9, len(heads), 8, BLOCK), jnp.float32),
        pltpu.VMEM((9, len(heads), 8, BLOCK), jnp.float32),
        pltpu.VMEM((2, 9, 8, BLOCK), jnp.float32),
        pltpu.SMEM((limit,), jnp.int32),
        pltpu.SMEM((limit,), jnp.int32),
        pltpu.SMEM((8,), jnp.int32),
    ]
    anywhere = pl.BlockSpec(memory_space=pl.ANY)
    vmem = pl.BlockSpec(memory_space=pltpu.VMEM)
    if last:
        out_specs = [anywhere] * 4
        out_shape = [jax.ShapeDtypeStruct((2, height + TAIL, BLOCK), jnp.bfloat16)] * 4
        scratch += [pltpu.VMEM((8, height + TAIL, BLOCK), jnp.bfloat16), pltpu.SemaphoreType.DMA((4,))]
    else:
        out_specs = [anywhere, vmem]
        out_shape = [
            jax.ShapeDtypeStruct((8, WIDTH, BLOCK), jnp.float32),
            jax.ShapeDtypeStruct((2, 8, 8, BLOCK), jnp.float32),
        ]
    return pl.pallas_call(
        functools.partial(attention, first_pair, pairs, split, start, last, heads),
        in_specs=[pl.BlockSpec(memory_space=pltpu.SMEM)]
        + ([] if start else [anywhere, vmem])
        + [pl.BlockSpec(memory_space=pltpu.HBM)] * (4 + len(sources)),
        out_specs=out_specs,
        scratch_shapes=scratch,
        out_shape=out_shape,
        cost_estimate=pl.CostEstimate(
            flops=3 * 10**9, transcendentals=pairs * 4 * 5 * BLOCK**2, bytes_accessed=pairs * 2**20
        ),
        compiler_params=pltpu.CompilerParams(vmem_limit_bytes=56 * 2**20),
    )(mask, *(state or ()), *queries, *sources)


def combine_kernel(heads, own, one, two, three, out):
    parts = (own, one, two, three)
    height = len(heads) * HD
    for b in range(2):
        lses = []
        for part in parts:
            table = part[b, height : height + TAIL, :].astype(jnp.float32)
            lses.append(table[0:8] + table[8:16] + table[16:24])
        peak = functools.reduce(jnp.maximum, lses)
        shares = [jnp.exp2(lse - peak) for lse in lses]
        whole = 1.0 / (shares[0] + shares[1] + shares[2] + shares[3])
        shares = [share * whole for share in shares]
        for k, h in enumerate(heads):
            rows = slice(k * HD, (k + 1) * HD)
            value = parts[0][b, rows, :].astype(jnp.float32) * shares[0][h : h + 1]
            for part, share in zip(parts[1:], shares[1:]):
                value = value + part[b, rows, :].astype(jnp.float32) * share[h : h + 1]
            out[b * BLOCK : (b + 1) * BLOCK, rows] = value.T.astype(jnp.bfloat16)


def combine(parts, heads):
    return pl.pallas_call(
        functools.partial(combine_kernel, heads), out_shape=jax.ShapeDtypeStruct((ROWS, len(heads) * HD), jnp.bfloat16)
    )(*parts)


def project_kernel(place_ref, a, b, c, d, w0, w1, w2, w3, *refs):
    gate, sofar, out, rows = refs if len(refs) == 4 else (None, None, *refs)
    for j, piece in enumerate((a, b, c, d)):
        rows[place_ref[j]] = piece[...]
    for i in range(out.shape[1] // 256):
        cols = slice(i * 256, (i + 1) * 256)
        value = None if sofar is None else sofar[:, cols]
        for j, weight in enumerate((w0, w1, w2, w3)):
            new = jnp.dot(rows[j], weight[:, cols], preferred_element_type=jnp.float32)
            value = new if value is None else value + new
        if gate is not None:
            value = gate[:, cols] * value
        out[:, cols] = value.astype(out.dtype)


def project(place, pieces, weights, *more):
    cols = weights[0].shape[1]
    vmem = pl.BlockSpec(memory_space=pltpu.VMEM)
    return pl.pallas_call(
        project_kernel,
        in_specs=[pl.BlockSpec(memory_space=pltpu.SMEM)] + [vmem] * (8 + len(more)),
        out_specs=vmem,
        scratch_shapes=[pltpu.VMEM((4, *pieces[0].shape), jnp.bfloat16)],
        out_shape=jax.ShapeDtypeStruct((ROWS, cols), jnp.bfloat16 if more else jnp.float32),
        name="project" if more else "project_first",
    )(place, *pieces, *weights, *more)


HALVES = {"a": (0, 1, 2), "b": (3, 4)}
CUT = len(HALVES["a"]) * HD


def stages(queries, keys, values, block_lists, list_counts, out_weight, gate):
    xlo, z, y = lax.axis_index("xlo"), lax.axis_index("z"), lax.axis_index("y")
    xhi, core = lax.axis_index("xhi"), lax.axis_index("core")

    own = prepare(keys, values)
    before, after, near = [own], [own], [own]
    near.append(swap_core(own))
    for d in (1, 2, 3):
        before.append(shift(before[-1], "z", 8, 1))
        after.append(shift(after[-1], "z", 8, -1))
        near += [before[d], swap_core(before[d])]
        near += [after[d], swap_core(after[d])]
    far_keys = shift(before[3][0], "z", 8, 1)
    far_values = shift(after[3][1], "z", 8, -1)
    far = [far_keys, far_values, swap_core(far_keys)]
    far.append(swap_core(far_values))

    top, bottom = out_weight[:CUT], out_weight[CUT:]
    t1 = shift(top, "y", 4, 1)
    b3 = shift(bottom, "y", 4, -1)
    b1 = shift(bottom, "y", 4, 1)
    t3 = shift(top, "y", 4, -1)
    t2 = shift(t1, "y", 4, 1)
    b2 = shift(b3, "y", 4, -1)
    weights = {"a": [top, t1, t2, t3], "b": [bottom, b1, b2, b3]}

    table = jnp.concatenate([block_lists, list_counts[:, None]], axis=1)
    tables, all_queries = [table], [queries]
    for r in (1, 2, 3):
        tables.append(shift_x(table, r))
        all_queries.append(shift_x(queries, r))
    tables = jnp.stack(tables).reshape(8, LIST + 1)

    steps = jnp.array([s for s, _ in SOURCES], jnp.int32)
    other = jnp.array([c for _, c in SOURCES], jnp.int32)
    quarter = 2 * xhi + jnp.bitwise_xor(other, core)
    first = ((xlo * 8 + (z + steps) % 8) * 4 + quarter) * 2
    ids = (first[:, None] + jnp.arange(2)[None, :]).reshape(-1)
    used = jnp.arange(LIST)[None, :] < tables[:, LIST:]
    mask = jnp.any((tables[:, :LIST, None] == ids[None, None, :]) & used[:, :, None], axis=1).astype(jnp.int32)

    state = attend(mask, all_queries, None, near[:6], 0, 6)
    state = attend(mask, all_queries, state, near[6:10], 6, 4)
    state = attend(mask, all_queries, state, near[10:], 10, 4)
    places = [(i, j) for i in range(4) for j in range(4)]
    groups = jnp.stack([2 * xhi + core, 2 * (1 - xhi) + core, 2 * xhi + 1 - core, 2 * (1 - xhi) + 1 - core])
    place = ((y - groups) % 4).astype(jnp.int32)
    gate = gate[None, :]

    result = ()
    for name, heads in HALVES.items():
        parts = attend(mask, all_queries, state, far, 14, 2, heads)
        back = [parts[0]]
        for r in (1, 2, 3):
            back.append(shift_x(parts[r], -r))
        attended = combine(back, heads)
        here = lax.ppermute(attended, ("y", "xhi", "core"), [(4 * i + j, 4 * j + i) for i, j in places])
        there = lax.ppermute(attended, ("y", "xhi", "core"), [(4 * i + j, 4 * j + (i ^ 2)) for i, j in places])
        pieces = [here, there, swap_core(here)]
        pieces.append(swap_core(there))
        result = project(place, pieces, weights[name], *result)
        result = (gate, result)
    return result[1]


def solution(mesh):
    fine = Mesh(mesh.devices.reshape(2, 8, 4, 2, 2), ("xlo", "z", "y", "xhi", "core"))
    rows, rep = ("xlo", "z", "xhi", "core"), ("xhi", "core")
    placed = (P(rows, "y"), P(rows, "y"), P(rows, "y"), P(rows, None), P(rows), P("y", rep), P(rep))
    return jax.shard_map(stages, mesh=fine, in_specs=placed, out_specs=P(("xlo", "z", "y"), rep), check_vma=False)
```

```python
import functools
import math

import jax
import jax.numpy as jnp
from jax import lax
from jax.experimental import pallas as pl
from jax.experimental.pallas import tpu as pltpu
from jax.sharding import Mesh, PartitionSpec as P


HD = 128
BLOCK = 128
LIST = 16
HEADS = 5
ROWS = 2 * BLOCK
WIDTH = HEADS * HD
TAIL = 32
EMPTY = -1e30
SCALE2 = math.log2(math.e) / HD**0.5

CALLS = [
    [(0, 0), (0, 1), (-1, 0), (1, 0)],
    [(-1, 1), (1, 1), (-2, 0), (2, 0)],
    [(-2, 1), (2, 1), (-3, 0), (3, 0)],
    [(-3, 1), (3, 1), (4, 0)],
    [(4, 1)],
]
AXES = ("xlo", "z", "y", "xhi", "core")


def shift(value, axes, size, steps):
    return lax.ppermute(value, axes, [(i, (i + steps) % size) for i in range(size)])


def shift_x(value, steps):
    at = [2 * (x % 2) + x // 2 for x in range(4)]
    return lax.ppermute(value, ("xlo", "xhi"), [(at[x], at[(x + steps) % 4]) for x in range(4)])


def swap_core(value):
    return lax.ppermute(value, "core", [(0, 1), (1, 0)])


def prepare_kernel(keys, values, out):
    for b in range(2):
        rows = slice(b * BLOCK, (b + 1) * BLOCK)
        for h in range(HEADS):
            cols = slice(h * HD, (h + 1) * HD)
            out[0, b * HEADS + h] = keys[rows, cols]
            out[1, b * HEADS + h] = values[rows, cols].T


def prepare(keys, values):
    return pl.pallas_call(
        prepare_kernel,
        out_shape=jax.ShapeDtypeStruct((2, 2 * HEADS, BLOCK, HD), jnp.bfloat16),
        name="prepare",
    )(keys, values)


def mark_kernel(source, target):
    target[0] = source[0]


def mark(place):
    smem = pl.BlockSpec(memory_space=pltpu.SMEM)
    return pl.pallas_call(
        mark_kernel, in_specs=[smem], out_specs=smem, out_shape=jax.ShapeDtypeStruct((1,), jnp.int32), name="mark"
    )(place)


def attention(number, split, start, last, place, *refs):
    refs = list(refs)
    masks, refs = refs[:4], refs[4:]
    if start:
        sent, refs = refs[:4], refs[4:]
    else:
        q, refs = refs[2], refs[3:]
    pairs = len(CALLS[number])
    sources, refs = refs[: sum(split)], refs[sum(split) :]
    if last:
        outs, refs = refs[:4], refs[4:]
        acc, ml, part, out_sems, refs = refs[0], refs[1], refs[2], refs[3], refs[4:]
    else:
        acc, ml, refs = refs[0], refs[1], refs[2:]
        if start:
            q, refs = refs[0], refs[1:]
    kv, sems, scores, tops, totals, codes, counts = refs

    copies, rest = [], list(sources)
    for i, pieces in enumerate(split):
        if pieces == 1:
            copies.append((rest.pop(0), kv.at[i]))
        else:
            copies += [(rest.pop(0), kv.at[i, 0]), (rest.pop(0), kv.at[i, 1])]
    if start:
        copies += [(source, q.at[i]) for i, source in enumerate(sent)]
    copies = [pltpu.make_async_copy(*copy, sems.at[i]) for i, copy in enumerate(copies)]
    for copy in copies:
        copy.start()

    me = place[0]
    xlo, z, xhi, core = me >> 7, (me >> 4) & 7, (me >> 1) & 1, me & 1
    ids = []
    for step, other in CALLS[number]:
        quarter = 2 * xhi + (1 - core if other else core)
        ids.append(((xlo * 8 + ((z + step) & 7)) * 4 + quarter) * 2)
    n = jnp.int32(0)
    for i in range(8):
        before = n
        for b in range(2 * pairs):
            codes[n] = jnp.int32(i * 64 + b)
            n = n + masks[i // 2][i % 2, ids[b // 2] + b % 2]
        counts[i] = n - before
    codes[n] = jnp.int32(8 * 64)
    trips = (n + 1) >> 1
    tops[...] = jnp.full(tops.shape, EMPTY, jnp.float32)
    totals[...] = jnp.zeros(totals.shape, jnp.float32)
    if start:
        acc[...] = jnp.zeros(acc.shape, jnp.float32)
        ml[0] = jnp.full(ml.shape[1:], EMPTY, jnp.float32)
        ml[1] = jnp.zeros(ml.shape[1:], jnp.float32)
    for copy in copies:
        copy.wait()

    def first_pass(j, carry):
        for u in range(2):
            i = 2 * j + u
            slot, b = codes[i] >> 6, codes[i] & 63
            at = slot & 7
            pair, tile = b >> 1, (b & 1) * HEADS
            q_rows = pl.ds(pl.multiple_of((at & 1) * BLOCK, BLOCK), BLOCK)
            for h in range(HEADS):
                s = (
                    lax.dot_general(
                        kv[pair, 0, tile + h],
                        q[at >> 1, q_rows, h * HD : (h + 1) * HD],
                        (((1,), (1,)), ((), ())),
                        preferred_element_type=jnp.float32,
                    )
                    * SCALE2
                )
                scores[i, h] = s
                tops[slot, h] = jnp.maximum(tops[slot, h], jnp.max(s.reshape(16, 8, BLOCK), axis=0))
        return carry

    lax.fori_loop(0, trips, first_pass, 0)
    line = lax.broadcasted_iota(jnp.int32, (8, BLOCK), 0)

    def middle(i, carry):
        @pl.when(counts[i] > 0)
        def _():
            old = ml[0, i]
            peak = old
            for h in range(HEADS):
                top = jnp.max(tops[i, h], axis=0, keepdims=True)
                peak = jnp.where(line == h, jnp.maximum(peak, top), peak)
            ml[0, i] = peak
            if not start:
                factor = jnp.exp2(old - peak)
                ml[1, i] = ml[1, i] * factor
                for h in range(HEADS):
                    rows = slice(h * HD, (h + 1) * HD)
                    acc[i, rows, :] = acc[i, rows, :] * factor[h : h + 1]

        return carry

    lax.fori_loop(0, 8, middle, 0)

    def second_pass(j, carry):
        for u in range(2):
            i = 2 * j + u
            slot, b = codes[i] >> 6, codes[i] & 63
            pair, tile = b >> 1, (b & 1) * HEADS
            for h in range(HEADS):
                rows = slice(h * HD, (h + 1) * HD)
                p = jnp.exp2(scores[i, h] - ml[0, slot, h : h + 1, :])
                totals[slot, h] = totals[slot, h] + jnp.sum(p.reshape(16, 8, BLOCK), axis=0)
                acc[slot, rows, :] = acc[slot, rows, :] + jnp.dot(
                    kv[pair, 1, tile + h], p.astype(jnp.bfloat16), preferred_element_type=jnp.float32
                )
        return carry

    lax.fori_loop(0, trips, second_pass, 0)

    def sums(i):
        weight = ml[1, i]
        for h in range(HEADS):
            total = jnp.sum(totals[i, h], axis=0, keepdims=True)
            weight = jnp.where(line == h, weight + total, weight)
        return weight

    if not last:

        def finish(i, carry):
            @pl.when(counts[i] > 0)
            def _():
                ml[1, i] = sums(i)

            return carry

        lax.fori_loop(0, 8, finish, 0)
        return

    leaves = []
    for r in range(4):
        for i in (2 * r, 2 * r + 1):
            weight = sums(i)
            some = weight > 0.0
            weight = jnp.where(some, weight, 1.0)
            lse = jnp.where(some, ml[0, i] + jnp.log2(weight), EMPTY)
            scale = 1.0 / weight
            for h in range(HEADS):
                rows = slice(h * HD, (h + 1) * HD)
                part[i, rows, :] = (acc[i, rows, :] * scale[h : h + 1]).astype(jnp.bfloat16)
            tables = []
            for _ in range(3):
                piece = lse.astype(jnp.bfloat16).astype(jnp.float32)
                tables.append(piece)
                lse = lse - piece
            tables.append(jnp.zeros((8, BLOCK), jnp.float32))
            part[i, WIDTH : WIDTH + TAIL, :] = jnp.concatenate(tables, axis=0).astype(jnp.bfloat16)
        leaves.append(pltpu.make_async_copy(part.at[2 * r : 2 * r + 2], outs[r], out_sems.at[r]))
        leaves[-1].start()
    for leave in leaves:
        leave.wait()


def attend(number, place, masks, state, sources):
    start, last = number == 0, number == len(CALLS) - 1
    split = [len(source) if isinstance(source, tuple) else 1 for source in sources]
    sources = [piece for source in sources for piece in (source if isinstance(source, tuple) else (source,))]
    pairs = len(CALLS[number])
    limit = 16 * pairs + 2
    scratch = [
        pltpu.VMEM((pairs, 2, 2 * HEADS, BLOCK, HD), jnp.bfloat16),
        pltpu.SemaphoreType.DMA((len(sources) + 4,)),
        pltpu.VMEM((limit, HEADS, BLOCK, BLOCK), jnp.float32),
        pltpu.VMEM((9, HEADS, 8, BLOCK), jnp.float32),
        pltpu.VMEM((9, HEADS, 8, BLOCK), jnp.float32),
        pltpu.SMEM((limit,), jnp.int32),
        pltpu.SMEM((8,), jnp.int32),
    ]
    hbm, vmem = pl.BlockSpec(memory_space=pltpu.HBM), pl.BlockSpec(memory_space=pltpu.VMEM)
    smem = pl.BlockSpec(memory_space=pltpu.SMEM)
    sums, statistics = ((9, WIDTH, BLOCK), jnp.float32), ((2, 9, 8, BLOCK), jnp.float32)
    aliases = {}
    if last:
        out_specs = [hbm] * 4
        out_shape = [jax.ShapeDtypeStruct((2, WIDTH + TAIL, BLOCK), jnp.bfloat16)] * 4
        scratch = [
            pltpu.VMEM((8, WIDTH + TAIL, BLOCK), jnp.bfloat16),
            pltpu.SemaphoreType.DMA((4,)),
        ] + scratch
        out_specs = out_specs + [vmem, vmem]
        out_shape = out_shape + [pltpu.VMEM(*sums), pltpu.VMEM(*statistics)]
        aliases = {5: 4, 6: 5}
    else:
        out_specs = [vmem, vmem]
        out_shape = [pltpu.VMEM(*sums), pltpu.VMEM(*statistics)]
        if start:
            out_specs.append(vmem)
            out_shape.append(pltpu.VMEM((4, ROWS, WIDTH), jnp.bfloat16))
        else:
            aliases = {5: 0, 6: 1}
    return pl.pallas_call(
        functools.partial(attention, number, split, start, last),
        in_specs=[smem] * 5 + ([hbm] * 4 if start else [vmem] * 3) + [hbm] * len(sources),
        out_specs=out_specs,
        scratch_shapes=scratch,
        out_shape=out_shape,
        input_output_aliases=aliases,
        cost_estimate=pl.CostEstimate(
            flops=2 * 10**9, transcendentals=pairs * 4 * 5 * BLOCK**2, bytes_accessed=pairs * 2**20
        ),
        compiler_params=pltpu.CompilerParams(vmem_limit_bytes=44 * 2**20),
    )(place, *masks, *state, *sources)


def combine_kernel(own, one, two, three, out):
    parts = (own, one, two, three)
    for b in range(2):
        lses = []
        for part in parts:
            table = part[b, WIDTH : WIDTH + TAIL, :].astype(jnp.float32)
            lses.append(table[0:8] + table[8:16] + table[16:24])
        peak = functools.reduce(jnp.maximum, lses)
        shares = [jnp.exp2(lse - peak) for lse in lses]
        whole = 1.0 / (shares[0] + shares[1] + shares[2] + shares[3])
        shares = [share * whole for share in shares]
        for h in range(HEADS):
            rows = slice(h * HD, (h + 1) * HD)
            value = parts[0][b, rows, :].astype(jnp.float32) * shares[0][h : h + 1]
            for part, share in zip(parts[1:], shares[1:]):
                value = value + part[b, rows, :].astype(jnp.float32) * share[h : h + 1]
            out[b * BLOCK : (b + 1) * BLOCK, rows] = value.T.astype(jnp.bfloat16)


def combine(parts):
    return pl.pallas_call(
        combine_kernel, out_shape=jax.ShapeDtypeStruct((ROWS, WIDTH), jnp.bfloat16), name="combine"
    )(*parts)


def project_kernel(place, a, b, c, d, t0, t1, t2, t3, b0, b1, b2, b3, gate, out, rows):
    me = place[0]
    y, rep = (me >> 2) & 3, me & 3
    for piece, group in ((a, rep), (b, rep ^ 2), (c, rep ^ 1), (d, rep ^ 3)):
        rows[(y - group) & 3] = piece[...]
    dot = functools.partial(jnp.dot, preferred_element_type=jnp.float32)
    for i in range(out.shape[1] // 256):
        cols = slice(i * 256, (i + 1) * 256)
        value = dot(rows[0, :, :CUT], t0[:, cols])
        for j, top in ((1, t1), (2, t2), (3, t3)):
            value = value + dot(rows[j, :, :CUT], top[:, cols])
        for j, bottom in enumerate((b0, b1, b2, b3)):
            value = value + dot(rows[j, :, CUT:], bottom[:, cols])
        out[:, cols] = (gate[:, cols] * value).astype(jnp.bfloat16)


def project(place, pieces, weights, gate):
    cols = weights[0].shape[1]
    vmem = pl.BlockSpec(memory_space=pltpu.VMEM)
    return pl.pallas_call(
        project_kernel,
        in_specs=[pl.BlockSpec(memory_space=pltpu.SMEM)] + [vmem] * 13,
        out_specs=vmem,
        scratch_shapes=[pltpu.VMEM((4, ROWS, WIDTH), jnp.bfloat16)],
        out_shape=jax.ShapeDtypeStruct((ROWS, cols), jnp.bfloat16),
        name="project",
    )(place, *pieces, *weights, gate[None, :])


CUT = 384


def stages(queries, keys, values, block_lists, list_counts, out_weight, gate):
    place = mark(lax.axis_index(AXES).astype(jnp.int32).reshape(1))

    own = prepare(keys, values)
    near = {(0, 0): own}
    near[0, 1] = swap_core(own)
    for sign in (1, -1):
        for d in (1, 2, 3):
            near[-sign * d, 0] = shift(near[-sign * (d - 1), 0], "z", 8, sign)
            near[-sign * d, 1] = swap_core(near[-sign * d, 0])
    far_keys = shift(near[-3, 0][0], "z", 8, 1)
    far_values = shift(near[3, 0][1], "z", 8, -1)
    near[4, 0] = (far_keys, far_values)
    far_keys = swap_core(far_keys)
    far_values = swap_core(far_values)
    near[4, 1] = (far_keys, far_values)

    top, bottom = out_weight[:CUT], out_weight[CUT:]
    t1 = shift(top, "y", 4, 1)
    b3 = shift(bottom, "y", 4, -1)
    b1 = shift(bottom, "y", 4, 1)
    t3 = shift(top, "y", 4, -1)
    t2 = shift(t1, "y", 4, 1)
    b2 = shift(b3, "y", 4, -1)

    used = jnp.arange(LIST)[None, :] < list_counts[:, None]
    listed = (block_lists[:, :, None] == jnp.arange(128)[None, None, :]) & used[:, :, None]
    mask = jnp.any(listed, axis=1).astype(jnp.int32)
    masks, state = [mask], [queries]
    for r in (1, 2, 3):
        masks.append(shift_x(mask, r))
        state.append(shift_x(queries, r))

    all_queries = None
    for number, call in enumerate(CALLS):
        result = attend(number, place, masks, state, [near[key] for key in call])
        if number == 0:
            all_queries = result[2]
        state = [result[0], result[1], all_queries]
    parts = result[:4]

    back = [parts[0]]
    for r in (1, 2, 3):
        back.append(shift_x(parts[r], -r))
    attended = combine(back)

    places = [(i, j) for i in range(4) for j in range(4)]
    here = lax.ppermute(attended, ("y", "xhi", "core"), [(4 * i + j, 4 * j + i) for i, j in places])
    there = lax.ppermute(attended, ("y", "xhi", "core"), [(4 * i + j, 4 * j + (i ^ 2)) for i, j in places])
    pieces = [here, there, swap_core(here)]
    pieces.append(swap_core(there))
    return project(place, pieces, [top, t1, t2, t3, bottom, b1, b2, b3], gate)


def solution(mesh):
    fine = Mesh(mesh.devices.reshape(2, 8, 4, 2, 2), AXES)
    rows, rep = ("xlo", "z", "xhi", "core"), ("xhi", "core")
    placed = (P(rows, "y"), P(rows, "y"), P(rows, "y"), P(rows, None), P(rows), P("y", rep), P(rep))
    return jax.shard_map(stages, mesh=fine, in_specs=placed, out_specs=P(("xlo", "z", "y"), rep), check_vma=False)
```

```python
import functools
import math

import jax
import jax.numpy as jnp
from jax import lax
from jax.experimental import pallas as pl
from jax.experimental.pallas import tpu as pltpu
from jax.sharding import Mesh, PartitionSpec as P


HD = 128
BLOCK = 128
LIST = 16
HEADS = 5
ROWS = 2 * BLOCK
WIDTH = HEADS * HD
TAIL = 32
EMPTY = -1e30
SCALE2 = math.log2(math.e) / HD**0.5

CALLS = [
    [(0, 0), (0, 1), (-1, 0), (1, 0)],
    [(-1, 1), (1, 1), (-2, 0), (2, 0)],
    [(-2, 1), (2, 1), (-3, 0), (3, 0)],
    [(-3, 1), (3, 1), (4, 0)],
    [(4, 1)],
]
AXES = ("xlo", "z", "y", "xhi", "core")


def shift(value, axes, size, steps):
    return lax.ppermute(value, axes, [(i, (i + steps) % size) for i in range(size)])


def shift_x(value, steps):
    at = [2 * (x % 2) + x // 2 for x in range(4)]
    return lax.ppermute(value, ("xlo", "xhi"), [(at[x], at[(x + steps) % 4]) for x in range(4)])


def swap_core(value):
    return lax.ppermute(value, "core", [(0, 1), (1, 0)])


def turn_kernel(values, out):
    for b in range(2):
        for h in range(HEADS):
            out[b * HEADS + h] = values[b * BLOCK : (b + 1) * BLOCK, h * HD : (h + 1) * HD].T


def turn(values):
    return pl.pallas_call(
        turn_kernel, out_shape=jax.ShapeDtypeStruct((2 * HEADS, HD, BLOCK), jnp.bfloat16), name="turn"
    )(values)


def mark_kernel(source, target):
    target[0] = source[0]


def mark(place):
    smem = pl.BlockSpec(memory_space=pltpu.SMEM)
    return pl.pallas_call(
        mark_kernel, in_specs=[smem], out_specs=smem, out_shape=jax.ShapeDtypeStruct((1,), jnp.int32), name="mark"
    )(place)


def attention(number, start, last, place, *refs):
    refs = list(refs)
    masks, refs = refs[:4], refs[4:]
    if start:
        sent, refs = refs[:4], refs[4:]
    else:
        q, refs = refs[2], refs[3:]
    pairs = len(CALLS[number])
    sources, refs = refs[: 2 * pairs], refs[2 * pairs :]
    if last:
        outs, refs = refs[:4], refs[4:]
        acc, ml, part, out_sems, refs = refs[0], refs[1], refs[2], refs[3], refs[4:]
    else:
        acc, ml, refs = refs[0], refs[1], refs[2:]
        if start:
            q, refs = refs[0], refs[1:]
    key_blocks, value_blocks, sems, scores, tops, totals, codes, counts = refs

    copies = [(source, key_blocks.at[i]) for i, source in enumerate(sources[::2])]
    copies += [(source, value_blocks.at[i]) for i, source in enumerate(sources[1::2])]
    if start:
        copies += [(source, q.at[i]) for i, source in enumerate(sent)]
    copies = [pltpu.make_async_copy(*copy, sems.at[i]) for i, copy in enumerate(copies)]
    for copy in copies:
        copy.start()

    me = place[0]
    xlo, z, xhi, core = me >> 7, (me >> 4) & 7, (me >> 1) & 1, me & 1
    ids = []
    for step, other in CALLS[number]:
        quarter = 2 * xhi + (1 - core if other else core)
        ids.append(((xlo * 8 + ((z + step) & 7)) * 4 + quarter) * 2)
    n = jnp.int32(0)
    for i in range(8):
        before = n
        for b in range(2 * pairs):
            codes[n] = jnp.int32(i * 64 + b)
            n = n + masks[i // 2][i % 2, ids[b // 2] + b % 2]
        counts[i] = n - before
    codes[n] = jnp.int32(8 * 64)
    trips = (n + 1) >> 1
    tops[...] = jnp.full(tops.shape, EMPTY, jnp.float32)
    totals[...] = jnp.zeros(totals.shape, jnp.float32)
    if start:
        acc[...] = jnp.zeros(acc.shape, jnp.float32)
        ml[0] = jnp.full(ml.shape[1:], EMPTY, jnp.float32)
        ml[1] = jnp.zeros(ml.shape[1:], jnp.float32)
    for copy in copies:
        copy.wait()

    def first_pass(j, carry):
        for u in range(2):
            i = 2 * j + u
            slot, b = codes[i] >> 6, codes[i] & 63
            at = slot & 7
            pair, k_rows = b >> 1, pl.ds(pl.multiple_of((b & 1) * BLOCK, BLOCK), BLOCK)
            q_rows = pl.ds(pl.multiple_of((at & 1) * BLOCK, BLOCK), BLOCK)
            for h in range(HEADS):
                s = (
                    lax.dot_general(
                        key_blocks[pair, k_rows, h * HD : (h + 1) * HD],
                        q[at >> 1, q_rows, h * HD : (h + 1) * HD],
                        (((1,), (1,)), ((), ())),
                        preferred_element_type=jnp.float32,
                    )
                    * SCALE2
                )
                scores[i, h] = s
                tops[slot, h] = jnp.maximum(tops[slot, h], jnp.max(s.reshape(16, 8, BLOCK), axis=0))
        return carry

    lax.fori_loop(0, trips, first_pass, 0)
    line = lax.broadcasted_iota(jnp.int32, (8, BLOCK), 0)

    def middle(i, carry):
        @pl.when(counts[i] > 0)
        def _():
            old = ml[0, i]
            peak = old
            for h in range(HEADS):
                top = jnp.max(tops[i, h], axis=0, keepdims=True)
                peak = jnp.where(line == h, jnp.maximum(peak, top), peak)
            ml[0, i] = peak
            if not start:
                factor = jnp.exp2(old - peak)
                ml[1, i] = ml[1, i] * factor
                for h in range(HEADS):
                    rows = slice(h * HD, (h + 1) * HD)
                    acc[i, rows, :] = acc[i, rows, :] * factor[h : h + 1]

        return carry

    lax.fori_loop(0, 8, middle, 0)

    def second_pass(j, carry):
        for u in range(2):
            i = 2 * j + u
            slot, b = codes[i] >> 6, codes[i] & 63
            pair, tile = b >> 1, (b & 1) * HEADS
            for h in range(HEADS):
                rows = slice(h * HD, (h + 1) * HD)
                p = jnp.exp2(scores[i, h] - ml[0, slot, h : h + 1, :])
                totals[slot, h] = totals[slot, h] + jnp.sum(p.reshape(16, 8, BLOCK), axis=0)
                acc[slot, rows, :] = acc[slot, rows, :] + jnp.dot(
                    value_blocks[pair, tile + h], p.astype(jnp.bfloat16), preferred_element_type=jnp.float32
                )
        return carry

    lax.fori_loop(0, trips, second_pass, 0)

    def sums(i):
        weight = ml[1, i]
        for h in range(HEADS):
            total = jnp.sum(totals[i, h], axis=0, keepdims=True)
            weight = jnp.where(line == h, weight + total, weight)
        return weight

    if not last:

        def finish(i, carry):
            @pl.when(counts[i] > 0)
            def _():
                ml[1, i] = sums(i)

            return carry

        lax.fori_loop(0, 8, finish, 0)
        return

    leaves = []
    for r in range(4):
        for i in (2 * r, 2 * r + 1):
            weight = sums(i)
            some = weight > 0.0
            weight = jnp.where(some, weight, 1.0)
            lse = jnp.where(some, ml[0, i] + jnp.log2(weight), EMPTY)
            scale = 1.0 / weight
            for h in range(HEADS):
                rows = slice(h * HD, (h + 1) * HD)
                part[i, rows, :] = (acc[i, rows, :] * scale[h : h + 1]).astype(jnp.bfloat16)
            tables = []
            for _ in range(3):
                piece = lse.astype(jnp.bfloat16).astype(jnp.float32)
                tables.append(piece)
                lse = lse - piece
            tables.append(jnp.zeros((8, BLOCK), jnp.float32))
            part[i, WIDTH : WIDTH + TAIL, :] = jnp.concatenate(tables, axis=0).astype(jnp.bfloat16)
        leaves.append(pltpu.make_async_copy(part.at[2 * r : 2 * r + 2], outs[r], out_sems.at[r]))
        leaves[-1].start()
    for leave in leaves:
        leave.wait()


def attend(number, place, masks, state, sources):
    start, last = number == 0, number == len(CALLS) - 1
    sources = [piece for source in sources for piece in source]
    pairs = len(CALLS[number])
    limit = 16 * pairs + 2
    scratch = [
        pltpu.VMEM((pairs, ROWS, WIDTH), jnp.bfloat16),
        pltpu.VMEM((pairs, 2 * HEADS, HD, BLOCK), jnp.bfloat16),
        pltpu.SemaphoreType.DMA((len(sources) + 4,)),
        pltpu.VMEM((limit, HEADS, BLOCK, BLOCK), jnp.float32),
        pltpu.VMEM((9, HEADS, 8, BLOCK), jnp.float32),
        pltpu.VMEM((9, HEADS, 8, BLOCK), jnp.float32),
        pltpu.SMEM((limit,), jnp.int32),
        pltpu.SMEM((8,), jnp.int32),
    ]
    hbm, vmem = pl.BlockSpec(memory_space=pltpu.HBM), pl.BlockSpec(memory_space=pltpu.VMEM)
    smem = pl.BlockSpec(memory_space=pltpu.SMEM)
    sums, statistics = ((9, WIDTH, BLOCK), jnp.float32), ((2, 9, 8, BLOCK), jnp.float32)
    aliases = {}
    if last:
        out_specs = [hbm] * 4
        out_shape = [jax.ShapeDtypeStruct((2, WIDTH + TAIL, BLOCK), jnp.bfloat16)] * 4
        scratch = [
            pltpu.VMEM((8, WIDTH + TAIL, BLOCK), jnp.bfloat16),
            pltpu.SemaphoreType.DMA((4,)),
        ] + scratch
        out_specs = out_specs + [vmem, vmem]
        out_shape = out_shape + [pltpu.VMEM(*sums), pltpu.VMEM(*statistics)]
        aliases = {5: 4, 6: 5}
    else:
        out_specs = [vmem, vmem]
        out_shape = [pltpu.VMEM(*sums), pltpu.VMEM(*statistics)]
        if start:
            out_specs.append(vmem)
            out_shape.append(pltpu.VMEM((4, ROWS, WIDTH), jnp.bfloat16))
        else:
            aliases = {5: 0, 6: 1}
    return pl.pallas_call(
        functools.partial(attention, number, start, last),
        in_specs=[smem] * 5 + ([hbm] * 4 if start else [vmem] * 3) + [hbm] * len(sources),
        out_specs=out_specs,
        scratch_shapes=scratch,
        out_shape=out_shape,
        input_output_aliases=aliases,
        cost_estimate=pl.CostEstimate(
            flops=2 * 10**9, transcendentals=pairs * 4 * 5 * BLOCK**2, bytes_accessed=pairs * 2**20
        ),
        compiler_params=pltpu.CompilerParams(vmem_limit_bytes=44 * 2**20),
    )(place, *masks, *state, *sources)


def combine_kernel(own, one, two, three, out):
    parts = (own, one, two, three)
    for b in range(2):
        lses = []
        for part in parts:
            table = part[b, WIDTH : WIDTH + TAIL, :].astype(jnp.float32)
            lses.append(table[0:8] + table[8:16] + table[16:24])
        peak = functools.reduce(jnp.maximum, lses)
        shares = [jnp.exp2(lse - peak) for lse in lses]
        whole = 1.0 / (shares[0] + shares[1] + shares[2] + shares[3])
        shares = [share * whole for share in shares]
        for h in range(HEADS):
            rows = slice(h * HD, (h + 1) * HD)
            value = parts[0][b, rows, :].astype(jnp.float32) * shares[0][h : h + 1]
            for part, share in zip(parts[1:], shares[1:]):
                value = value + part[b, rows, :].astype(jnp.float32) * share[h : h + 1]
            out[b * BLOCK : (b + 1) * BLOCK, rows] = value.T.astype(jnp.bfloat16)


def combine(parts):
    return pl.pallas_call(
        combine_kernel,
        out_shape=jax.ShapeDtypeStruct((ROWS, WIDTH), jnp.bfloat16),
        compiler_params=pltpu.CompilerParams(vmem_limit_bytes=16 * 2**20),
        name="combine",
    )(*parts)


def pack_kernel(place, w0, w1, w2, w2b, w3, out, sems):
    me = place[0]
    y, rep = (me >> 2) & 3, me & 3
    copies = []
    for r, low, weight in ((0, 0, w0), (1, 0, w1), (2, 0, w2), (2, CUT, w2b), (3, 0, w3)):
        row = (((y - r) & 3) ^ rep) * WIDTH + low
        target = out.at[pl.ds(pl.multiple_of(row, HD), weight.shape[0])]
        copies.append(pltpu.make_async_copy(weight, target, sems.at[len(copies)]))
    for copy in copies:
        copy.start()
    for copy in copies:
        copy.wait()


def pack(place, weights):
    hbm, vmem = pl.BlockSpec(memory_space=pltpu.HBM), pl.BlockSpec(memory_space=pltpu.VMEM)
    return pl.pallas_call(
        pack_kernel,
        in_specs=[pl.BlockSpec(memory_space=pltpu.SMEM)] + [hbm] * len(weights),
        out_specs=vmem,
        scratch_shapes=[pltpu.SemaphoreType.DMA((len(weights),))],
        out_shape=pltpu.VMEM((4 * WIDTH, weights[0].shape[1]), jnp.bfloat16),
        compiler_params=pltpu.CompilerParams(vmem_limit_bytes=2 * 2**20),
        name="pack",
    )(place, *weights)


def project_kernel(a, b, c, d, weight, gate, out, rows, sems):
    copies = []
    for k, piece in enumerate((a, b, c, d)):
        copies.append(pltpu.make_async_copy(piece, rows.at[:, k * WIDTH : (k + 1) * WIDTH], sems.at[k]))
        copies[-1].start()
    for copy in copies:
        copy.wait()

    def tile(i, carry):
        cols = pl.ds(pl.multiple_of(i * 256, 256), 256)
        value = jnp.dot(rows[...], weight[:, cols], preferred_element_type=jnp.float32)
        out[:, cols] = (gate[:, cols] * value).astype(jnp.bfloat16)
        return carry

    lax.fori_loop(0, out.shape[1] // 256, tile, 0)


def project(pieces, weight, gate):
    hbm, vmem = pl.BlockSpec(memory_space=pltpu.HBM), pl.BlockSpec(memory_space=pltpu.VMEM)
    return pl.pallas_call(
        project_kernel,
        in_specs=[hbm] * 4 + [vmem] * 2,
        out_specs=vmem,
        scratch_shapes=[pltpu.VMEM((ROWS, 4 * WIDTH), jnp.bfloat16), pltpu.SemaphoreType.DMA((4,))],
        out_shape=jax.ShapeDtypeStruct((ROWS, weight.shape[1]), jnp.bfloat16),
        compiler_params=pltpu.CompilerParams(vmem_limit_bytes=24 * 2**20),
        name="project",
    )(*pieces, weight, gate)


CUT = 384


def stages(queries, keys, values, block_lists, list_counts, out_weight, gate):
    place = mark(lax.axis_index(AXES).astype(jnp.int32).reshape(1))

    turned = turn(values)
    held = {"k": {(0, 0): keys}, "v": {(0, 0): turned}}
    for name, near in held.items():
        near[0, 1] = swap_core(near[0, 0])
        for sign in (1, -1):
            for d in (1, 2, 3):
                near[-sign * d, 0] = shift(near[-sign * (d - 1), 0], "z", 8, sign)
                near[-sign * d, 1] = swap_core(near[-sign * d, 0])
        sign = 1 if name == "k" else -1
        near[4, 0] = shift(near[-sign * 3, 0], "z", 8, sign)
        near[4, 1] = swap_core(near[4, 0])

    w1 = shift(out_weight, "y", 4, 1)
    w3 = shift(out_weight, "y", 4, -1)
    w2 = shift(w1[:CUT], "y", 4, 1)
    w2b = shift(w3[CUT:], "y", 4, -1)
    weight = pack(place, [out_weight, w1, w2, w2b, w3])

    used = jnp.arange(LIST)[None, :] < list_counts[:, None]
    listed = (block_lists[:, :, None] == jnp.arange(128)[None, None, :]) & used[:, :, None]
    mask = jnp.any(listed, axis=1).astype(jnp.int32)
    masks, state = [mask], [queries]
    for r in (1, 2, 3):
        masks.append(shift_x(mask, r))
        state.append(shift_x(queries, r))

    all_queries = None
    for number, call in enumerate(CALLS):
        result = attend(number, place, masks, state, [(held["k"][key], held["v"][key]) for key in call])
        if number == 0:
            all_queries = result[2]
        state = [result[0], result[1], all_queries]
    parts = result[:4]

    back = [parts[0]]
    for r in (1, 2, 3):
        back.append(shift_x(parts[r], -r))
    attended = combine(back)

    places = [(i, j) for i in range(4) for j in range(4)]
    here = lax.ppermute(attended, ("y", "xhi", "core"), [(4 * i + j, 4 * j + i) for i, j in places])
    there = lax.ppermute(attended, ("y", "xhi", "core"), [(4 * i + j, 4 * j + (i ^ 2)) for i, j in places])
    pieces = [here, swap_core(here), there]
    pieces.append(swap_core(there))
    return project(pieces, weight, gate[None, :])


def solution(mesh):
    fine = Mesh(mesh.devices.reshape(2, 8, 4, 2, 2), AXES)
    rows, rep = ("xlo", "z", "xhi", "core"), ("xhi", "core")
    placed = (P(rows, "y"), P(rows, "y"), P(rows, "y"), P(rows, None), P(rows), P("y", rep), P(rep))
    return jax.shard_map(stages, mesh=fine, in_specs=placed, out_specs=P(("xlo", "z", "y"), rep), check_vma=False)
```
